32 devices in a mesh: role: 4 (over x, core), shard: 8 (over z, y).
Axes of the slice: x: 2, y: 2, z: 4, core: 2. Of those that a mesh axis runs over, the one named last changes fastest.
Arguments:
- action_ids: int32 [32, 8], P(('role', 'shard')), may hold values from 0 to 255
- traj_lengths: int32 [32], P(('role', 'shard')), may hold values from 1 to 8
- action_table: bfloat16 [256, 4096], P(None, 'shard'), may hold values from -6 to 6
- prefix_keys: bfloat16 [32, 128, 2048], P(('role', 'shard')), may hold values from -6 to 6
- prefix_values: bfloat16 [32, 128, 2048], P(('role', 'shard')), may hold values from -6 to 6
- qkv_weight: bfloat16 [4096, 6144], P('shard'), may hold values from -0.09375 to 0.09375
- out_weight: bfloat16 [2048, 4096], P(None, 'shard'), may hold values from -0.125 to 0.125
- first_qkv: float32 [4096, 6144], P('shard', 'role'), may hold values from -6 to 6
- second_qkv: float32 [4096, 6144], P('shard', 'role'), may hold values from 1 to 100
- first_out: float32 [2048, 4096], P('role', 'shard'), may hold values from -6 to 6
- second_out: float32 [2048, 4096], P('role', 'shard'), may hold values from 1 to 100
- out_cotangent: bfloat16 [256, 4096], P('role', 'shard'), may hold values from -6 to 6
Outputs:
- decoded: bfloat16 [256, 4096], P('role', 'shard')
- new_qkv: bfloat16 [4096, 6144], P('shard')
- new_out: bfloat16 [2048, 4096], P(None, 'shard')
- moment_qkv: float32 [4096, 6144], P('shard', 'role')
- square_qkv: float32 [4096, 6144], P('shard', 'role')
- moment_out: float32 [2048, 4096], P('role', 'shard')
- square_out: float32 [2048, 4096], P('role', 'shard')
The draws below stay inside these ranges and needn't reach their ends.
All inputs are finite; a program needn't handle non-finite values.
Results may differ from the reference program's by a relative error of at most 0.0071.
Values may be sent and summed in bfloat16 or wider, within the bound.
No kernel may reach another device: no remote copies, remote signals or barrier semaphores. Data moves between devices by JAX's collectives and lax.ppermute only.
A program may use at most 128 MiB of HBM per device.

```python
import math
import jax
import jax.numpy as jnp
from jax import lax

D = 4096
HD = 128
BINS = 256
PREFIX = 128
TRAJ = 8
HW = 2048
EPIS = 32
ROWS = 256
N_ROLE = 4


def plant(array, own_key, least, largest):
    dims = array.shape
    place = [jax.random.randint(jax.random.fold_in(own_key, axis), (), 0, dims[axis]) for axis in range(len(dims))]
    array = array.at[tuple(place)].set(least)
    longest = dims.index(max(dims))
    place[longest] = (place[longest] + 1) % dims[longest]
    return array.at[tuple(place)].set(largest)


def shard_levels(key, extent, split, smallest, high):
    def one(dim, parts):
        steps = jax.random.uniform(jax.random.fold_in(jax.random.fold_in(key, 6), dim), (parts,), jnp.float32, smallest / len(split), high / len(split))
        return jnp.repeat(jnp.exp(steps), extent[dim] // parts).reshape((-1,) + (1,) * (len(extent) - dim - 1))

    gain = one(*split[0])
    for cut in split[1:]:
        gain = gain * one(*cut)
    return gain


def normal_values(rng, extent, width, most, pieces=(), kind=jnp.bfloat16):
    entries = width * jax.random.normal(rng, extent, jnp.float32)
    if pieces:
        entries = entries * shard_levels(rng, extent, pieces, -0.22, 0.18)
    return jnp.clip(entries, -most, most).astype(kind)


def setup_inputs(seed: int = 0) -> dict:
    splits = jax.random.split(jax.random.key(seed), 13)
    return {
        "action_ids": plant(jax.random.randint(splits[0], (EPIS, TRAJ), 0, BINS), jax.random.fold_in(splits[0], 1), 0, BINS - 1).astype(jnp.int32),
        "traj_lengths": plant(jax.random.randint(splits[1], (EPIS,), 1, TRAJ + 1), jax.random.fold_in(splits[1], 1), 1, TRAJ).astype(jnp.int32),
        "action_table": normal_values(splits[2], (BINS, D), 1.0, 6.0, ((1, 8),)),
        "prefix_keys": normal_values(splits[3], (EPIS, PREFIX, HW), 1.0, 6.0, ((0, 32),)),
        "prefix_values": normal_values(splits[4], (EPIS, PREFIX, HW), 1.0, 6.0, ((0, 32),)),
        "qkv_weight": normal_values(splits[5], (D, 3 * HW), D ** -0.5, 0.09375, ((0, 8),)),
        "out_weight": normal_values(splits[6], (HW, D), HW ** -0.5, 0.125, ((1, 8),)),
        "first_qkv": normal_values(splits[7], (D, 3 * HW), 1.0, 6.0, ((0, 8), (1, 4)), jnp.float32),
        "second_qkv": jnp.clip(jnp.exp(math.log(100.0) - 4.6051702 * jax.random.uniform(splits[8], (D, 3 * HW), jnp.float32) ** shard_levels(splits[8], (D, 3 * HW), ((0, 8), (1, 4)), -0.2, 0.2)), 1.0, 100.0),
        "first_out": normal_values(splits[9], (HW, D), 1.0, 6.0, ((0, 4), (1, 8)), jnp.float32),
        "second_out": jnp.clip(jnp.exp(math.log(100.0) - 4.6051702 * jax.random.uniform(splits[10], (HW, D), jnp.float32) ** shard_levels(splits[10], (HW, D), ((0, 4), (1, 8)), -0.2, 0.2)), 1.0, 100.0),
        "out_cotangent": normal_values(splits[11], (ROWS, D), 1.0, 6.0, ((0, 4), (1, 8))),
    }


learn_rate = 0.001
first_decay = 0.9
second_decay = 0.95
adam_eps = 1e-08
weight_decay = 0.1
first_fix = 1.0 - 0.9 ** 10
second_fix = 1.0 - 0.95 ** 10

def unpack(qkv_rows, keys_pre, vals_pre):
    span_width = keys_pre.shape[-1]
    head_count = span_width // HD
    positions = qkv_rows.shape[0]
    total_keys = keys_pre.shape[0] + positions
    queries = qkv_rows[:, :span_width].astype(jnp.float32).reshape(positions, head_count, HD)
    all_keys = jnp.concatenate([keys_pre, qkv_rows[:, span_width:2 * span_width]], 0).astype(jnp.float32).reshape(total_keys, head_count, HD)
    all_values = jnp.concatenate([vals_pre, qkv_rows[:, 2 * span_width:]], 0).astype(jnp.float32).reshape(total_keys, head_count, HD)
    return (queries, all_keys, all_values)

def attend(qkv_rows, keys_pre, vals_pre, length):
    queries, all_keys, all_values = unpack(qkv_rows, keys_pre, vals_pre)
    prefix_len = keys_pre.shape[0]
    positions = qkv_rows.shape[0]
    attn_scale = HD ** (-0.5)
    scores = jnp.einsum('thd,lhd->htl', queries, all_keys) * attn_scale
    position = jnp.arange(positions, dtype=jnp.int32)[:, None]
    offset = jnp.arange(prefix_len + positions, dtype=jnp.int32)[None, :] - prefix_len
    allowed = (offset < 0) | (offset <= position) & (offset < length)
    scores = jnp.where(allowed[None], scores, -1e+30)
    weights = jax.nn.softmax(scores, axis=-1)
    rounded = lax.optimization_barrier(weights.astype(jnp.bfloat16))
    head_mix = jnp.einsum('htl,lhd->thd', rounded.astype(jnp.float32), all_values)
    return (head_mix.reshape(positions, -1).astype(jnp.bfloat16), weights, rounded)

def attend_back(qkv_rows, keys_pre, vals_pre, weights, rounded, upstream):
    queries, all_keys, all_values = unpack(qkv_rows, keys_pre, vals_pre)
    prefix_len = keys_pre.shape[0]
    positions = qkv_rows.shape[0]
    attn_scale = HD ** (-0.5)
    grads_head = upstream.astype(jnp.float32).reshape(positions, -1, HD)
    grad_weights = jnp.einsum('thd,lhd->htl', grads_head, all_values)
    grad_scores = weights * (grad_weights - lax.optimization_barrier(jnp.sum(weights * grad_weights, axis=-1, keepdims=True))) * attn_scale
    grad_rounded = lax.optimization_barrier(grad_scores.astype(jnp.bfloat16)).astype(jnp.float32)
    grad_query = jnp.einsum('htl,lhd->thd', grad_rounded, all_keys).reshape(positions, -1)
    grad_key = jnp.einsum('htl,thd->lhd', grad_rounded[:, :, prefix_len:], queries).reshape(positions, -1)
    grad_value = jnp.einsum('htl,thd->lhd', rounded.astype(jnp.float32)[:, :, prefix_len:], grads_head).reshape(positions, -1)
    return jnp.concatenate([grad_query, grad_key, grad_value], 1).astype(jnp.bfloat16)

def adamw(params, gradient, first_moment, second_moment):
    moment_one = first_decay * first_moment + (1.0 - first_decay) * gradient
    moment_two = second_decay * second_moment + (1.0 - second_decay) * gradient * gradient
    stepped = moment_one / first_fix / (jnp.sqrt(moment_two / second_fix) + adam_eps)
    wide_params = params.astype(jnp.float32)
    updated = wide_params - learn_rate * (stepped + weight_decay * wide_params)
    return (updated, moment_one, moment_two)

def reference(action_ids, traj_lengths, action_table, prefix_keys, prefix_values, qkv_weight, out_weight, first_qkv, second_qkv, first_out, second_out, out_cotangent):
    episodes = action_ids.shape[0]
    horizon = action_ids.shape[1]
    contract_rows = (((0,), (0,)), ((), ()))
    onehot = (action_ids.reshape(-1)[:, None] == jnp.arange(BINS, dtype=jnp.int32)[None, :]).astype(jnp.bfloat16)
    inputs = jnp.dot(onehot, action_table, preferred_element_type=jnp.float32).astype(jnp.bfloat16)
    projected = jnp.dot(inputs, qkv_weight, preferred_element_type=jnp.float32).astype(jnp.bfloat16).reshape(episodes, horizon, -1)
    head_mix, weights, rounded = jax.vmap(attend)(projected, prefix_keys, prefix_values, traj_lengths)
    head_rows = head_mix.reshape(episodes * horizon, -1)
    decoded = jnp.dot(head_rows, out_weight, preferred_element_type=jnp.float32).astype(jnp.bfloat16)
    first_ep = (N_ROLE - 1) * episodes // N_ROLE
    first_row = first_ep * horizon
    valid = (jnp.arange(horizon, dtype=jnp.int32)[None, :] < traj_lengths[:, None]).reshape(-1)
    masked = jnp.where(valid[:, None], out_cotangent, jnp.zeros_like(out_cotangent))[first_row:]
    grad_out = lax.dot_general(head_rows[first_row:], masked, contract_rows, preferred_element_type=jnp.float32)
    grad_heads = lax.dot_general(masked, out_weight, (((1,), (1,)), ((), ())), preferred_element_type=jnp.float32).astype(jnp.bfloat16)
    grad_heads = grad_heads.reshape(episodes - first_ep, horizon, -1)
    grad_proj = jax.vmap(attend_back)(projected[first_ep:], prefix_keys[first_ep:], prefix_values[first_ep:], weights[first_ep:], rounded[first_ep:], grad_heads)
    grad_proj = grad_proj.reshape((episodes - first_ep) * horizon, -1)
    grad_qkv = lax.dot_general(inputs[first_row:], grad_proj, contract_rows, preferred_element_type=jnp.float32)
    new_qkv, moment_qkv, square_qkv = adamw(qkv_weight, grad_qkv, first_qkv, second_qkv)
    new_out, moment_out, square_out = adamw(out_weight, grad_out, first_out, second_out)
    return (decoded, new_qkv.astype(jnp.bfloat16), new_out.astype(jnp.bfloat16), moment_qkv, square_qkv, moment_out, square_out)
```

```python
import jax
import jax.numpy as jnp
from jax import lax
from jax.sharding import PartitionSpec as P

HD = 128


learn_rate = 0.001
first_decay = 0.9
second_decay = 0.95
adam_eps = 1e-08
weight_decay = 0.1
first_fix = 1.0 - 0.9**10
second_fix = 1.0 - 0.95**10


def unpack(qkv_rows, keys_pre, vals_pre):
    span_width = keys_pre.shape[-1]
    head_count = span_width // HD
    positions = qkv_rows.shape[0]
    total_keys = keys_pre.shape[0] + positions
    queries = qkv_rows[:, :span_width].astype(jnp.float32).reshape(positions, head_count, HD)
    all_keys = (
        jnp.concatenate([keys_pre, qkv_rows[:, span_width : 2 * span_width]], 0)
        .astype(jnp.float32)
        .reshape(total_keys, head_count, HD)
    )
    all_values = (
        jnp.concatenate([vals_pre, qkv_rows[:, 2 * span_width :]], 0)
        .astype(jnp.float32)
        .reshape(total_keys, head_count, HD)
    )
    return (queries, all_keys, all_values)


def attend(qkv_rows, keys_pre, vals_pre, length):
    queries, all_keys, all_values = unpack(qkv_rows, keys_pre, vals_pre)
    prefix_len = keys_pre.shape[0]
    positions = qkv_rows.shape[0]
    attn_scale = HD ** (-0.5)
    scores = jnp.einsum("thd,lhd->htl", queries, all_keys) * attn_scale
    position = jnp.arange(positions, dtype=jnp.int32)[:, None]
    offset = jnp.arange(prefix_len + positions, dtype=jnp.int32)[None, :] - prefix_len
    allowed = (offset < 0) | (offset <= position) & (offset < length)
    scores = jnp.where(allowed[None], scores, -1e30)
    weights = jax.nn.softmax(scores, axis=-1)
    rounded = lax.optimization_barrier(weights.astype(jnp.bfloat16))
    head_mix = jnp.einsum("htl,lhd->thd", rounded.astype(jnp.float32), all_values)
    return (head_mix.reshape(positions, -1).astype(jnp.bfloat16), weights, rounded)


def attend_back(qkv_rows, keys_pre, vals_pre, weights, rounded, upstream):
    queries, all_keys, all_values = unpack(qkv_rows, keys_pre, vals_pre)
    prefix_len = keys_pre.shape[0]
    positions = qkv_rows.shape[0]
    attn_scale = HD ** (-0.5)
    grads_head = upstream.astype(jnp.float32).reshape(positions, -1, HD)
    grad_weights = jnp.einsum("thd,lhd->htl", grads_head, all_values)
    grad_scores = (
        weights
        * (grad_weights - jnp.sum(weights * grad_weights, axis=-1, keepdims=True))
        * attn_scale
    )
    grad_rounded = lax.optimization_barrier(grad_scores.astype(jnp.bfloat16)).astype(jnp.float32)
    grad_query = jnp.einsum("htl,lhd->thd", grad_rounded, all_keys).reshape(positions, -1)
    grad_key = jnp.einsum("htl,thd->lhd", grad_rounded[:, :, prefix_len:], queries).reshape(
        positions, -1
    )
    grad_value = jnp.einsum(
        "htl,thd->lhd", rounded.astype(jnp.float32)[:, :, prefix_len:], grads_head
    ).reshape(positions, -1)
    return jnp.concatenate([grad_query, grad_key, grad_value], 1).astype(jnp.bfloat16)


def adamw(params, gradient, first_moment, second_moment):
    moment_one = first_decay * first_moment + (1.0 - first_decay) * gradient
    moment_two = second_decay * second_moment + (1.0 - second_decay) * gradient * gradient
    stepped = moment_one / first_fix / (jnp.sqrt(moment_two / second_fix) + adam_eps)
    wide_params = params.astype(jnp.float32)
    updated = wide_params - learn_rate * (stepped + weight_decay * wide_params)
    return (updated, moment_one, moment_two)


def shards(
    action_ids,
    traj_lengths,
    action_table,
    prefix_keys,
    prefix_values,
    qkv_weight,
    out_weight,
    first_qkv,
    second_qkv,
    first_out,
    second_out,
    out_cotangent,
):
    f32, bf16 = jnp.float32, jnp.bfloat16
    episodes, horizon = action_ids.shape
    rows = episodes * horizon
    roles, parts = lax.axis_size("role"), lax.axis_size("shard")
    role, part = lax.axis_index("role"), lax.axis_index("shard")
    learner = roles - 1
    is_learner = role == learner
    contract_rows = (((0,), (0,)), ((), ()))

    def ring(k):
        return [(i, (i + k) % parts) for i in range(parts)]

    def gather_turned(x):
        return jnp.concatenate([x] + [lax.ppermute(x, "shard", ring(k)) for k in range(1, parts)], 0)

    def turn(x):
        blocks = x.reshape(parts, rows, -1)[::-1]
        twice = jnp.concatenate([blocks, blocks], 0)
        return lax.dynamic_slice_in_dim(twice, parts - 1 - part, parts, 0).reshape(x.shape)

    def scatter_sum(partial, only=None):
        pieces = partial.astype(bf16)
        total = partial[:rows]
        for k in range(1, parts):
            piece = pieces[(parts - k) * rows : (parts - k + 1) * rows]
            if only is None:
                got = lax.ppermute(piece, "shard", ring(k))
            else:
                pairs = [(only * parts + a, only * parts + b) for a, b in ring(k)]
                got = lax.ppermute(piece, ("role", "shard"), pairs)
            total = total + got.astype(f32)
        return total.astype(bf16)

    def from_learner(pieces):
        mine = pieces[learner]
        got = None
        for q in range(learner):
            part_q = lax.ppermute(pieces[q], "role", [(learner, q)])
            got = part_q if got is None else got + part_q
        return jnp.where(is_learner, mine, got)

    turned_cot = turn(out_cotangent)
    grad_partial = lax.dot_general(
        turned_cot, out_weight, (((1,), (1,)), ((), ())), preferred_element_type=f32
    )
    grad_heads = scatter_sum(grad_partial, learner)

    ids = gather_turned(action_ids)
    onehot = (
        ids.reshape(-1)[:, None] == jnp.arange(action_table.shape[0], dtype=jnp.int32)[None, :]
    ).astype(bf16)
    inputs = jnp.dot(onehot, action_table, preferred_element_type=f32).astype(bf16)
    projected = scatter_sum(jnp.dot(inputs, qkv_weight, preferred_element_type=f32))
    learner_side = from_learner([jnp.concatenate([inputs, turned_cot], 1)] * roles)
    learner_inputs = learner_side[:, : inputs.shape[1]]
    learner_cot = learner_side[:, inputs.shape[1] :]

    projected = projected.reshape(episodes, horizon, -1)
    head_mix, weights, rounded = jax.vmap(attend)(
        projected, prefix_keys, prefix_values, traj_lengths
    )
    head_rows = head_mix.reshape(rows, -1)
    valid = (jnp.arange(horizon, dtype=jnp.int32)[None, :] < traj_lengths[:, None]).reshape(-1)
    grad_heads = jnp.where(valid[:, None], grad_heads, jnp.zeros_like(grad_heads))
    masked_rows = jnp.where(valid[:, None], head_rows, jnp.zeros_like(head_rows))
    grad_proj = jax.vmap(attend_back)(
        projected,
        prefix_keys,
        prefix_values,
        weights,
        rounded,
        grad_heads.reshape(episodes, horizon, -1),
    ).reshape(rows, -1)

    qkv_part = first_qkv.shape[1]
    out_part = first_out.shape[0]
    wanted = [
        jnp.concatenate(
            [
                grad_proj[:, q * qkv_part : (q + 1) * qkv_part],
                masked_rows[:, q * out_part : (q + 1) * out_part],
            ],
            1,
        )
        for q in range(roles)
    ]
    learner_rows = gather_turned(from_learner(wanted))
    grad_qkv = lax.dot_general(
        learner_inputs, learner_rows[:, :qkv_part], contract_rows, preferred_element_type=f32
    )
    grad_out = lax.dot_general(
        learner_rows[:, qkv_part:], learner_cot, contract_rows, preferred_element_type=f32
    )

    weight_qkv = lax.dynamic_slice_in_dim(qkv_weight, role * qkv_part, qkv_part, 1)
    weight_out = lax.dynamic_slice_in_dim(out_weight, role * out_part, out_part, 0)
    piece_qkv, moment_qkv, square_qkv = adamw(weight_qkv, grad_qkv, first_qkv, second_qkv)
    piece_out, moment_out, square_out = adamw(weight_out, grad_out, first_out, second_out)

    def collect(piece, axis):
        held = {0: piece.astype(bf16)}
        bit = roles // 2
        while bit:
            swap = [(i, i ^ bit) for i in range(roles)]
            held.update({d | bit: lax.ppermute(x, "role", swap) for d, x in list(held.items())})
            bit //= 2
        by_distance = [held[d] for d in range(roles)]
        blocks = [lax.select_n(role ^ q, *by_distance) for q in range(roles)]
        return jnp.concatenate(blocks, axis)

    new_qkv = collect(piece_qkv, 1)
    new_out = collect(piece_out, 0)

    gathered = gather_turned(head_rows)
    decoded = turn(jnp.dot(gathered, out_weight, preferred_element_type=f32).astype(bf16))
    return (decoded, new_qkv, new_out, moment_qkv, square_qkv, moment_out, square_out)


def solution(mesh):
    in_specs = (
        P(("role", "shard"), None),
        P(("role", "shard")),
        P(None, "shard"),
        P(("role", "shard"), None, None),
        P(("role", "shard"), None, None),
        P("shard", None),
        P(None, "shard"),
        P("shard", "role"),
        P("shard", "role"),
        P("role", "shard"),
        P("role", "shard"),
        P("role", "shard"),
    )
    out_specs = (
        P("role", "shard"),
        P("shard", None),
        P(None, "shard"),
        P("shard", "role"),
        P("shard", "role"),
        P("role", "shard"),
        P("role", "shard"),
    )
    return jax.shard_map(shards, mesh=mesh, in_specs=in_specs, out_specs=out_specs, check_vma=False)
```

```python
import functools

import jax
import jax.numpy as jnp
from jax import lax
from jax.experimental import pallas as pl
from jax.experimental.pallas import tpu as pltpu
from jax.sharding import PartitionSpec as P


HD = 128


learn_rate = 0.001
first_decay = 0.9
second_decay = 0.95
adam_eps = 1e-08
weight_decay = 0.1
first_fix = 1.0 - 0.9**10
second_fix = 1.0 - 0.95**10


def unpack(qkv_rows, keys_pre, vals_pre):
    span_width = keys_pre.shape[-1]
    head_count = span_width // HD
    positions = qkv_rows.shape[0]
    total_keys = keys_pre.shape[0] + positions
    queries = qkv_rows[:, :span_width].astype(jnp.float32).reshape(positions, head_count, HD)
    all_keys = (
        jnp.concatenate([keys_pre, qkv_rows[:, span_width : 2 * span_width]], 0)
        .astype(jnp.float32)
        .reshape(total_keys, head_count, HD)
    )
    all_values = (
        jnp.concatenate([vals_pre, qkv_rows[:, 2 * span_width :]], 0)
        .astype(jnp.float32)
        .reshape(total_keys, head_count, HD)
    )
    return (queries, all_keys, all_values)


def attend(qkv_rows, keys_pre, vals_pre, length):
    queries, all_keys, all_values = unpack(qkv_rows, keys_pre, vals_pre)
    prefix_len = keys_pre.shape[0]
    positions = qkv_rows.shape[0]
    attn_scale = HD ** (-0.5)
    scores = jnp.einsum("thd,lhd->htl", queries, all_keys) * attn_scale
    position = jnp.arange(positions, dtype=jnp.int32)[:, None]
    offset = jnp.arange(prefix_len + positions, dtype=jnp.int32)[None, :] - prefix_len
    allowed = (offset < 0) | (offset <= position) & (offset < length)
    scores = jnp.where(allowed[None], scores, -1e30)
    weights = jax.nn.softmax(scores, axis=-1)
    rounded = lax.optimization_barrier(weights.astype(jnp.bfloat16))
    head_mix = jnp.einsum("htl,lhd->thd", rounded.astype(jnp.float32), all_values)
    return (head_mix.reshape(positions, -1).astype(jnp.bfloat16), weights, rounded)


def attend_back(qkv_rows, keys_pre, vals_pre, weights, rounded, upstream):
    queries, all_keys, all_values = unpack(qkv_rows, keys_pre, vals_pre)
    prefix_len = keys_pre.shape[0]
    positions = qkv_rows.shape[0]
    attn_scale = HD ** (-0.5)
    grads_head = upstream.astype(jnp.float32).reshape(positions, -1, HD)
    grad_weights = jnp.einsum("thd,lhd->htl", grads_head, all_values)
    grad_scores = (
        weights
        * (grad_weights - jnp.sum(weights * grad_weights, axis=-1, keepdims=True))
        * attn_scale
    )
    grad_rounded = lax.optimization_barrier(grad_scores.astype(jnp.bfloat16)).astype(jnp.float32)
    grad_query = jnp.einsum("htl,lhd->thd", grad_rounded, all_keys).reshape(positions, -1)
    grad_key = jnp.einsum("htl,thd->lhd", grad_rounded[:, :, prefix_len:], queries).reshape(
        positions, -1
    )
    grad_value = jnp.einsum(
        "htl,thd->lhd", rounded.astype(jnp.float32)[:, :, prefix_len:], grads_head
    ).reshape(positions, -1)
    return jnp.concatenate([grad_query, grad_key, grad_value], 1).astype(jnp.bfloat16)


def pack_body(first_ref, second_ref, out_ref):
    width = out_ref.shape[1] // 2
    out_ref[:, :width] = first_ref[...].astype(out_ref.dtype)
    out_ref[:, width:] = second_ref[...].astype(out_ref.dtype)


def pack(first, second, width):
    depth = first.shape[0]
    steps = 2
    spec = pl.BlockSpec((depth // steps, width), lambda i: (i, 0))
    return pl.pallas_call(
        pack_body,
        grid=(steps,),
        in_specs=[spec, spec],
        out_specs=pl.BlockSpec((depth // steps, 2 * width), lambda i: (i, 0)),
        out_shape=jax.ShapeDtypeStruct((depth, 2 * width), jnp.bfloat16),
        cost_estimate=pl.CostEstimate(flops=0, bytes_accessed=12 * depth * width, transcendentals=0),
        name="pack",
    )(first, second)


def stack_body(edges, *refs):
    count = len(refs) - len(edges) + 1
    rows = refs[0].shape[0]
    for i in range(count):
        for j, out in enumerate(refs[count:]):
            out[i * rows : (i + 1) * rows, :] = refs[i][:, edges[j] : edges[j + 1]]


def stack(blocks, cuts):
    edges = [sum(cuts[:i]) for i in range(len(cuts) + 1)]
    height = len(blocks) * blocks[0].shape[0]
    return pl.pallas_call(
        functools.partial(stack_body, edges),
        out_shape=[jax.ShapeDtypeStruct((height, c), blocks[0].dtype) for c in cuts],
        name="stack",
    )(*blocks)


def parcel_body(plan, *refs):
    outs = refs[-len(plan) :]
    for out, takes in zip(outs, plan):
        at = 0
        for which, begin, end in takes:
            out[:, at : at + end - begin] = refs[which][:, begin:end]
            at += end - begin


def parcel(sources, plan):
    return pl.pallas_call(
        functools.partial(parcel_body, plan),
        out_shape=[
            jax.ShapeDtypeStruct(
                (sources[0].shape[0], sum(e - b for _, b, e in takes)), sources[0].dtype
            )
            for takes in plan
        ],
        name="parcel",
    )(*sources)


def adamw_folded(params, gradient, first_moment, second_moment):
    moment_one = first_decay * first_moment + (1.0 - first_decay) * gradient
    moment_two = second_decay * second_moment + (1.0 - second_decay) * gradient * gradient
    fixed = moment_two * (1.0 / second_fix)
    stepped = (moment_one * (learn_rate / first_fix)) / (fixed * lax.rsqrt(fixed) + adam_eps)
    updated = params.astype(jnp.float32) * (1.0 - learn_rate * weight_decay) - stepped
    return (updated, moment_one, moment_two)


def update_body(aliased, role_ref, left_ref, right_ref, w_ref, m_ref, v_ref, *refs):
    grad_ref = refs[-1]
    outs = refs[aliased:-1]
    grad_ref[...] = lax.dot_general(
        left_ref[...], right_ref[...], (((0,), (0,)), ((), ())), preferred_element_type=jnp.float32
    )
    strip = 16

    def one(i, carry):
        at = pl.ds(pl.multiple_of(i * strip, strip), strip)
        updated, moment, square = adamw_folded(
            w_ref[at, :],
            grad_ref[at, :],
            m_ref[at, :].astype(jnp.float32),
            v_ref[at, :].astype(jnp.float32),
        )
        outs[0][at, :] = updated.astype(outs[0].dtype)
        if len(outs) > 1:
            outs[1][at, :] = moment
            outs[2][at, :] = square
        return carry

    lax.fori_loop(0, w_ref.shape[0] // strip, one, 0, unroll=2)


def update_blocks(role, left, right, weight, first, second, spots, shape, block, moments=None, keep=True):
    height, width = block
    grid = (shape[0] // height, shape[1] // width)
    depth = left.shape[0]
    at = {k: (lambda f: lambda i, j, p: f(i, j))(f) for k, f in spots.items() if k != "weight"}
    in_specs = [
        pl.BlockSpec((depth, height), at["left"]),
        pl.BlockSpec((depth, width), at["right"]),
        pl.BlockSpec(block, lambda i, j, p: spots["weight"](i, j, p[0])),
        pl.BlockSpec(block, at["first"]),
        pl.BlockSpec(block, at["second"]),
    ]
    out_specs = [pl.BlockSpec(block, lambda i, j, p: (i, j))]
    out_shape = [jax.ShapeDtypeStruct(shape, jnp.bfloat16)]
    operands = [left, right, weight, first, second]
    aliases = {}
    if keep:
        out_specs += [pl.BlockSpec(block, at["first"])] * 2
        out_shape += [jax.ShapeDtypeStruct(first.shape, jnp.float32)] * 2
        if moments is not None:
            operands += list(moments)
            in_specs += [pl.BlockSpec(memory_space=pl.ANY)] * 2
            aliases = {6: 1, 7: 2}
    size = shape[0] * shape[1]
    return pl.pallas_call(
        functools.partial(update_body, len(aliases)),
        grid_spec=pltpu.PrefetchScalarGridSpec(
            num_scalar_prefetch=1,
            grid=grid,
            in_specs=in_specs,
            out_specs=out_specs,
            scratch_shapes=[pltpu.VMEM(block, jnp.float32)],
        ),
        out_shape=out_shape,
        input_output_aliases=aliases,
        cost_estimate=pl.CostEstimate(
            flops=2 * depth * size, bytes_accessed=(20 if keep else 8) * size, transcendentals=2 * size
        ),
        name="update",
    )(role.reshape(1).astype(jnp.int32), *operands)


def join_body(role_ref, *refs):
    roles = refs[-1].shape[0]
    early, late, outs = refs[:roles], refs[roles : 2 * roles], refs[2 * roles : 3 * roles]
    qkv_ref, out_ref = refs[-2:]
    first, rest = early[0].shape[1], late[0].shape[1]
    for d in range(roles):
        owner = role_ref[0] ^ d
        qkv_ref[:, pl.ds(pl.multiple_of(owner * (first + rest), 128), first)] = early[d][...]
        qkv_ref[:, pl.ds(pl.multiple_of(owner * (first + rest) + first, 128), rest)] = late[d][...]
        out_ref[owner] = outs[d][...]


def join(role, early, late, outs):
    roles = len(outs)
    depth = early[0].shape[0]
    width = early[0].shape[1] + late[0].shape[1]
    out_rows, out_width = outs[0].shape
    steps = 2
    pieces = [*early, *late, *outs]
    new_qkv, new_out = pl.pallas_call(
        join_body,
        grid=(steps,),
        in_specs=[pl.BlockSpec(memory_space=pltpu.SMEM)]
        + [pl.BlockSpec((x.shape[0] // steps, x.shape[1]), lambda i: (i, 0)) for x in pieces],
        out_specs=[
            pl.BlockSpec((depth // steps, roles * width), lambda i: (i, 0)),
            pl.BlockSpec((roles, out_rows // steps, out_width), lambda i: (0, i, 0)),
        ],
        out_shape=[
            jax.ShapeDtypeStruct((depth, roles * width), jnp.bfloat16),
            jax.ShapeDtypeStruct((roles, out_rows, out_width), jnp.bfloat16),
        ],
        cost_estimate=pl.CostEstimate(
            flops=0, bytes_accessed=4 * roles * (depth * width + out_rows * out_width), transcendentals=0
        ),
        name="join",
    )(role.reshape(1).astype(jnp.int32), *pieces)
    return new_qkv, new_out.reshape(roles * out_rows, out_width)


def update(
    action_ids,
    traj_lengths,
    action_table,
    prefix_keys,
    prefix_values,
    qkv_weight,
    out_weight,
    first_qkv,
    second_qkv,
    first_out,
    second_out,
    out_cotangent,
):
    f32, bf16 = jnp.float32, jnp.bfloat16
    episodes, horizon = action_ids.shape
    rows = episodes * horizon
    roles, parts = lax.axis_size("role"), lax.axis_size("shard")
    role, part = lax.axis_index("role"), lax.axis_index("shard")
    learner = roles - 1
    is_learner = role == learner
    far = roles // 2
    qkv_part = first_qkv.shape[1]
    out_part = first_out.shape[0]
    head_width = prefix_keys.shape[-1]
    early_width = qkv_part // 3 * 2

    def hop(x, k):
        return lax.ppermute(x, "shard", [(i, i ^ k) for i in range(parts)])

    def gather_turned(x):
        return jnp.concatenate([x] + [hop(x, k) for k in range(1, parts)], 0)

    spot = jnp.arange(parts * rows, dtype=jnp.int32)
    turn_matrix = ((spot[:, None] ^ (part * rows)) == spot[None, :]).astype(bf16)

    def turn(x):
        return jnp.dot(turn_matrix, x, preferred_element_type=f32).astype(x.dtype)

    def swap(x, bit):
        return lax.ppermute(x, "role", [(i, i ^ bit) for i in range(roles)])

    far_moments = swap(pack(first_qkv, second_qkv, early_width), far)

    ids = gather_turned(action_ids)

    turned_cot = turn(out_cotangent)
    grad_partial = lax.dot_general(
        turned_cot, out_weight, (((1,), (1,)), ((), ())), preferred_element_type=f32
    )

    def inputs_of(bins):
        onehot = (
            bins.reshape(-1)[:, None] == jnp.arange(action_table.shape[0], dtype=jnp.int32)[None, :]
        ).astype(bf16)
        return jnp.dot(onehot, action_table, preferred_element_type=f32).astype(bf16)

    partial = jnp.concatenate(
        [jnp.dot(inputs_of(ids), qkv_weight, preferred_element_type=f32), grad_partial], 1
    )
    total = partial[:rows]
    pieces = partial[rows:].astype(bf16)
    for k in range(1, parts):
        total = total + hop(pieces[(k - 1) * rows : k * rows], k).astype(f32)
    total = total.astype(bf16)

    near_cot = jnp.where(is_learner, turned_cot, swap(turned_cot, 1))
    learner_cot = jnp.where(role >= far, near_cot, swap(near_cot, far))

    projected = total[:, : 3 * head_width].reshape(episodes, horizon, -1)
    grad_heads = total[:, 3 * head_width :]
    head_mix, weights, rounded = jax.vmap(attend)(
        projected, prefix_keys, prefix_values, traj_lengths
    )
    head_rows = head_mix.reshape(rows, -1)
    valid = (jnp.arange(horizon, dtype=jnp.int32)[None, :] < traj_lengths[:, None]).reshape(-1)
    grad_heads = jnp.where(valid[:, None], grad_heads, jnp.zeros_like(grad_heads))
    masked_rows = jnp.where(valid[:, None], head_rows, jnp.zeros_like(head_rows))
    grad_proj = jax.vmap(attend_back)(
        projected,
        prefix_keys,
        prefix_values,
        weights,
        rounded,
        grad_heads.reshape(episodes, horizon, -1),
    ).reshape(rows, -1)

    id_column = jnp.broadcast_to(action_ids.reshape(rows, 1).astype(bf16), (rows, 128))

    def wanted(q):
        own, other = q * qkv_part, (q ^ far) * qkv_part
        return (
            (0, own, own + qkv_part),
            (0, other, other + early_width),
            (1, q * out_part, (q + 1) * out_part),
            (1, (q ^ far) * out_part, ((q ^ far) + 1) * out_part),
            (2, 0, 128),
        )

    parcels = parcel([grad_proj, masked_rows, id_column], tuple(wanted(q) for q in range(roles)))
    mine = None
    for q in range(learner):
        got = lax.ppermute(parcels[q], "role", [(learner, q)])
        mine = got if mine is None else mine + got
    mine = jnp.where(is_learner, parcels[learner], mine)
    mine = jnp.concatenate([mine, head_rows], 1)
    moments_out = jnp.concatenate([first_out.astype(bf16), second_out.astype(bf16)], 0)
    far_moments_out = swap(moments_out, far)
    blocks = [mine] + [hop(mine, k) for k in range(1, parts)]
    cuts = [qkv_part, early_width, out_part, out_part, 128, head_width]
    own_rows, far_rows, own_mixed, far_mixed, learner_ids, gathered = stack(blocks, cuts)
    learner_inputs = inputs_of(learner_ids[:, 0].astype(jnp.int32))

    third = qkv_part - early_width
    high = min(256, first_qkv.shape[0])

    def spots(at, moved, weight):
        return {
            "left": lambda i, j: (0, i),
            "right": lambda i, j: (0, at + j),
            "first": lambda i, j: (i, at + j),
            "second": lambda i, j: (i, at + j + moved),
            "weight": weight,
        }

    late, moment_qkv, square_qkv = update_blocks(
        role, learner_inputs, own_rows, qkv_weight, first_qkv, second_qkv,
        spots(2, 0, lambda i, j, r: (i, r * 3 + 2 + j)), (first_qkv.shape[0], third), (high, third),
    )
    far_late = swap(late, far)
    near_late = swap(late, 1)
    piece_qkv, moment_qkv, square_qkv = update_blocks(
        role, learner_inputs, own_rows, qkv_weight, first_qkv, second_qkv,
        spots(0, 0, lambda i, j, r: (i, r * 3 + j)), (first_qkv.shape[0], early_width), (high, third),
        moments=(moment_qkv, square_qkv),
    )
    late_done = late
    (piece_far,) = update_blocks(
        role, learner_inputs, far_rows, qkv_weight, far_moments, far_moments,
        spots(0, 2, lambda i, j, r: (i, (r ^ far) * 3 + j)), (first_qkv.shape[0], early_width), (high, third), keep=False,
    )
    near_far = swap(piece_far, 1)
    tall = min(256, out_part)
    stories = out_part // tall
    (far_out,) = update_blocks(
        role, far_mixed, learner_cot, out_weight, far_moments_out, far_moments_out,
        {
            **spots(0, 0, lambda i, j, r: ((r ^ far) * stories + i, j)),
            "second": lambda i, j: (i + stories, j),
        },
        (out_part, first_out.shape[1]), (tall, first_out.shape[1]), keep=False,
    )
    piece_out, moment_out, square_out = update_blocks(
        role, own_mixed, learner_cot, out_weight, first_out, second_out,
        spots(0, 0, lambda i, j, r: (r * stories + i, j)), (out_part, first_out.shape[1]), (tall, first_out.shape[1]),
    )
    near_qkv = swap(piece_qkv, 1)
    near_out = swap(piece_out, 1)
    near_far_out = swap(far_out, 1)
    diagonal_late = swap(far_late, 1)
    new_qkv, new_out = join(
        role,
        [piece_qkv, near_qkv, piece_far, near_far],
        [late_done, near_late, far_late, diagonal_late],
        [piece_out, near_out, far_out, near_far_out],
    )

    decoded = turn(jnp.dot(gathered, out_weight, preferred_element_type=f32).astype(bf16))
    return (decoded, new_qkv, new_out, moment_qkv, square_qkv, moment_out, square_out)


def solution(mesh):
    in_specs = (
        P(("role", "shard"), None),
        P(("role", "shard")),
        P(None, "shard"),
        P(("role", "shard"), None, None),
        P(("role", "shard"), None, None),
        P("shard", None),
        P(None, "shard"),
        P("shard", "role"),
        P("shard", "role"),
        P("role", "shard"),
        P("role", "shard"),
        P("role", "shard"),
    )
    out_specs = (
        P("role", "shard"),
        P("shard", None),
        P(None, "shard"),
        P("shard", "role"),
        P("shard", "role"),
        P("role", "shard"),
        P("role", "shard"),
    )
    return jax.shard_map(update, mesh=mesh, in_specs=in_specs, out_specs=out_specs, check_vma=False)
```

```python
import functools

import jax
import jax.numpy as jnp
from jax import lax
from jax.experimental import pallas as pl
from jax.experimental.pallas import tpu as pltpu
from jax.sharding import PartitionSpec as P


HD = 128


learn_rate = 0.001
first_decay = 0.9
second_decay = 0.95
adam_eps = 1e-08
weight_decay = 0.1
first_fix = 1.0 - 0.9**10
second_fix = 1.0 - 0.95**10


def unpack(qkv_rows, keys_pre, vals_pre):
    span_width = keys_pre.shape[-1]
    head_count = span_width // HD
    positions = qkv_rows.shape[0]
    total_keys = keys_pre.shape[0] + positions
    queries = qkv_rows[:, :span_width].astype(jnp.float32).reshape(positions, head_count, HD)
    all_keys = (
        jnp.concatenate([keys_pre, qkv_rows[:, span_width : 2 * span_width]], 0)
        .astype(jnp.float32)
        .reshape(total_keys, head_count, HD)
    )
    all_values = (
        jnp.concatenate([vals_pre, qkv_rows[:, 2 * span_width :]], 0)
        .astype(jnp.float32)
        .reshape(total_keys, head_count, HD)
    )
    return (queries, all_keys, all_values)


def attend(qkv_rows, keys_pre, vals_pre, length):
    queries, all_keys, all_values = unpack(qkv_rows, keys_pre, vals_pre)
    prefix_len = keys_pre.shape[0]
    positions = qkv_rows.shape[0]
    attn_scale = HD ** (-0.5)
    scores = jnp.einsum("thd,lhd->htl", queries, all_keys) * attn_scale
    position = jnp.arange(positions, dtype=jnp.int32)[:, None]
    offset = jnp.arange(prefix_len + positions, dtype=jnp.int32)[None, :] - prefix_len
    allowed = (offset < 0) | (offset <= position) & (offset < length)
    scores = jnp.where(allowed[None], scores, -1e30)
    weights = jax.nn.softmax(scores, axis=-1)
    rounded = lax.optimization_barrier(weights.astype(jnp.bfloat16))
    head_mix = jnp.einsum("htl,lhd->thd", rounded.astype(jnp.float32), all_values)
    return (head_mix.reshape(positions, -1).astype(jnp.bfloat16), weights, rounded)


def attend_back(qkv_rows, keys_pre, vals_pre, weights, rounded, upstream):
    queries, all_keys, all_values = unpack(qkv_rows, keys_pre, vals_pre)
    prefix_len = keys_pre.shape[0]
    positions = qkv_rows.shape[0]
    attn_scale = HD ** (-0.5)
    grads_head = upstream.astype(jnp.float32).reshape(positions, -1, HD)
    grad_weights = jnp.einsum("thd,lhd->htl", grads_head, all_values)
    grad_scores = (
        weights
        * (grad_weights - jnp.sum(weights * grad_weights, axis=-1, keepdims=True))
        * attn_scale
    )
    grad_rounded = lax.optimization_barrier(grad_scores.astype(jnp.bfloat16)).astype(jnp.float32)
    grad_query = jnp.einsum("htl,lhd->thd", grad_rounded, all_keys).reshape(positions, -1)
    grad_key = jnp.einsum("htl,thd->lhd", grad_rounded[:, :, prefix_len:], queries).reshape(
        positions, -1
    )
    grad_value = jnp.einsum(
        "htl,thd->lhd", rounded.astype(jnp.float32)[:, :, prefix_len:], grads_head
    ).reshape(positions, -1)
    return jnp.concatenate([grad_query, grad_key, grad_value], 1).astype(jnp.bfloat16)


def pack_body(first_ref, second_ref, out_ref):
    width = out_ref.shape[1] // 2
    out_ref[:, :width] = first_ref[...].astype(out_ref.dtype)
    out_ref[:, width:] = second_ref[...].astype(out_ref.dtype)


def pack(first, second, width):
    depth = first.shape[0]
    steps = 2
    spec = pl.BlockSpec((depth // steps, width), lambda i: (i, 0))
    return pl.pallas_call(
        pack_body,
        grid=(steps,),
        in_specs=[spec, spec],
        out_specs=pl.BlockSpec((depth // steps, 2 * width), lambda i: (i, 0)),
        out_shape=jax.ShapeDtypeStruct((depth, 2 * width), jnp.bfloat16),
        cost_estimate=pl.CostEstimate(flops=0, bytes_accessed=12 * depth * width, transcendentals=0),
        name="pack",
    )(first, second)


def stack_body(edges, *refs):
    count = len(refs) - len(edges) + 1
    rows = refs[0].shape[0]
    for i in range(count):
        for j, out in enumerate(refs[count:]):
            out[i * rows : (i + 1) * rows, :] = refs[i][:, edges[j] : edges[j + 1]]


def stack(blocks, cuts):
    edges = [sum(cuts[:i]) for i in range(len(cuts) + 1)]
    height = len(blocks) * blocks[0].shape[0]
    return pl.pallas_call(
        functools.partial(stack_body, edges),
        out_shape=[jax.ShapeDtypeStruct((height, c), blocks[0].dtype) for c in cuts],
        name="stack",
    )(*blocks)


def parcel_body(plan, *refs):
    outs = refs[-len(plan) :]
    for out, takes in zip(outs, plan):
        at = 0
        for which, begin, end in takes:
            out[:, at : at + end - begin] = refs[which][:, begin:end]
            at += end - begin


def parcel(sources, plan):
    return pl.pallas_call(
        functools.partial(parcel_body, plan),
        out_shape=[
            jax.ShapeDtypeStruct(
                (sources[0].shape[0], sum(e - b for _, b, e in takes)), sources[0].dtype
            )
            for takes in plan
        ],
        name="parcel",
    )(*sources)


def adamw_folded(params, gradient, first_moment, second_moment):
    moment_one = first_decay * first_moment + (1.0 - first_decay) * gradient
    moment_two = second_decay * second_moment + (1.0 - second_decay) * gradient * gradient
    fixed = moment_two * (1.0 / second_fix)
    stepped = (moment_one * (learn_rate / first_fix)) / (fixed * lax.rsqrt(fixed) + adam_eps)
    updated = params.astype(jnp.float32) * (1.0 - learn_rate * weight_decay) - stepped
    return (updated, moment_one, moment_two)


def update_body(aliased, role_ref, left_ref, right_ref, w_ref, m_ref, v_ref, *refs):
    grad_ref = refs[-1]
    outs = refs[aliased:-1]
    grad_ref[...] = lax.dot_general(
        left_ref[...], right_ref[...], (((0,), (0,)), ((), ())), preferred_element_type=jnp.float32
    )
    strip = 16

    def one(i, carry):
        at = pl.ds(pl.multiple_of(i * strip, strip), strip)
        updated, moment, square = adamw_folded(
            w_ref[at, :],
            grad_ref[at, :],
            m_ref[at, :].astype(jnp.float32),
            v_ref[at, :].astype(jnp.float32),
        )
        outs[0][at, :] = updated.astype(outs[0].dtype)
        if len(outs) > 1:
            outs[1][at, :] = moment
            outs[2][at, :] = square
        return carry

    lax.fori_loop(0, w_ref.shape[0] // strip, one, 0, unroll=2)


def update_blocks(role, left, right, weight, first, second, spots, shape, block, moments=None, keep=True):
    height, width = block
    grid = (shape[0] // height, shape[1] // width)
    depth = left.shape[0]
    at = {k: (lambda f: lambda i, j, p: f(i, j))(f) for k, f in spots.items() if k != "weight"}
    in_specs = [
        pl.BlockSpec((depth, height), at["left"]),
        pl.BlockSpec((depth, width), at["right"]),
        pl.BlockSpec(block, lambda i, j, p: spots["weight"](i, j, p[0])),
        pl.BlockSpec(block, at["first"]),
        pl.BlockSpec(block, at["second"]),
    ]
    out_specs = [pl.BlockSpec(block, lambda i, j, p: (i, j))]
    out_shape = [jax.ShapeDtypeStruct(shape, jnp.bfloat16)]
    operands = [left, right, weight, first, second]
    aliases = {}
    if keep:
        out_specs += [pl.BlockSpec(block, at["first"])] * 2
        out_shape += [jax.ShapeDtypeStruct(first.shape, jnp.float32)] * 2
        if moments is not None:
            operands += list(moments)
            in_specs += [pl.BlockSpec(memory_space=pl.ANY)] * 2
            aliases = {6: 1, 7: 2}
    size = shape[0] * shape[1]
    return pl.pallas_call(
        functools.partial(update_body, len(aliases)),
        grid_spec=pltpu.PrefetchScalarGridSpec(
            num_scalar_prefetch=1,
            grid=grid,
            in_specs=in_specs,
            out_specs=out_specs,
            scratch_shapes=[pltpu.VMEM(block, jnp.float32)],
        ),
        out_shape=out_shape,
        input_output_aliases=aliases,
        cost_estimate=pl.CostEstimate(
            flops=2 * depth * size, bytes_accessed=(20 if keep else 8) * size, transcendentals=2 * size
        ),
        name="update",
    )(role.reshape(1).astype(jnp.int32), *operands)


def join_body(role_ref, *refs):
    roles = refs[-1].shape[0]
    early, late, outs = refs[:roles], refs[roles : 2 * roles], refs[2 * roles : 3 * roles]
    qkv_ref, out_ref = refs[-2:]
    first, rest = early[0].shape[1], late[0].shape[1]
    for d in range(roles):
        owner = role_ref[0] ^ d
        qkv_ref[:, pl.ds(pl.multiple_of(owner * (first + rest), 128), first)] = early[d][...]
        qkv_ref[:, pl.ds(pl.multiple_of(owner * (first + rest) + first, 128), rest)] = late[d][...]
        out_ref[owner] = outs[d][...]


def join(role, early, late, outs):
    roles = len(outs)
    depth = early[0].shape[0]
    width = early[0].shape[1] + late[0].shape[1]
    out_rows, out_width = outs[0].shape
    steps = 2
    pieces = [*early, *late, *outs]
    new_qkv, new_out = pl.pallas_call(
        join_body,
        grid=(steps,),
        in_specs=[pl.BlockSpec(memory_space=pltpu.SMEM)]
        + [pl.BlockSpec((x.shape[0] // steps, x.shape[1]), lambda i: (i, 0)) for x in pieces],
        out_specs=[
            pl.BlockSpec((depth // steps, roles * width), lambda i: (i, 0)),
            pl.BlockSpec((roles, out_rows // steps, out_width), lambda i: (0, i, 0)),
        ],
        out_shape=[
            jax.ShapeDtypeStruct((depth, roles * width), jnp.bfloat16),
            jax.ShapeDtypeStruct((roles, out_rows, out_width), jnp.bfloat16),
        ],
        cost_estimate=pl.CostEstimate(
            flops=0, bytes_accessed=4 * roles * (depth * width + out_rows * out_width), transcendentals=0
        ),
        name="join",
    )(role.reshape(1).astype(jnp.int32), *pieces)
    return new_qkv, new_out.reshape(roles * out_rows, out_width)


def update(
    action_ids,
    traj_lengths,
    action_table,
    prefix_keys,
    prefix_values,
    qkv_weight,
    out_weight,
    first_qkv,
    second_qkv,
    first_out,
    second_out,
    out_cotangent,
):
    f32, bf16 = jnp.float32, jnp.bfloat16
    episodes, horizon = action_ids.shape
    rows = episodes * horizon
    roles, parts = lax.axis_size("role"), lax.axis_size("shard")
    role, part = lax.axis_index("role"), lax.axis_index("shard")
    learner = roles - 1
    is_learner = role == learner
    far = roles // 2
    qkv_part = first_qkv.shape[1]
    out_part = first_out.shape[0]
    head_width = prefix_keys.shape[-1]
    early_width = qkv_part // 3 * 2

    def hop(x, k):
        return lax.ppermute(x, "shard", [(i, i ^ k) for i in range(parts)])

    def gather_turned(x):
        return jnp.concatenate([x] + [hop(x, k) for k in range(1, parts)], 0)

    spot = jnp.arange(parts * rows, dtype=jnp.int32)
    turn_matrix = ((spot[:, None] ^ (part * rows)) == spot[None, :]).astype(bf16)

    def turn(x):
        return jnp.dot(turn_matrix, x, preferred_element_type=f32).astype(x.dtype)

    def swap(x, bit):
        return lax.ppermute(x, "role", [(i, i ^ bit) for i in range(roles)])

    far_moments = swap(pack(first_qkv, second_qkv, early_width), far)

    ids = gather_turned(action_ids)

    turned_cot = turn(out_cotangent)
    grad_partial = lax.dot_general(
        turned_cot, out_weight, (((1,), (1,)), ((), ())), preferred_element_type=f32
    )

    def inputs_of(bins):
        onehot = (
            bins.reshape(-1)[:, None] == jnp.arange(action_table.shape[0], dtype=jnp.int32)[None, :]
        ).astype(bf16)
        return jnp.dot(onehot, action_table, preferred_element_type=f32).astype(bf16)

    inputs = inputs_of(ids)
    partial = jnp.concatenate(
        [jnp.dot(inputs, qkv_weight, preferred_element_type=f32), grad_partial], 1
    )
    total = partial[:rows]
    pieces = partial[rows:].astype(bf16)
    got = [hop(pieces[(k - 1) * rows : k * rows], k) for k in range(1, parts)]

    side = jnp.concatenate([inputs, turned_cot], 1)
    near_side = swap(side, 1)
    near_side = jnp.where(is_learner, side, near_side)
    near_side, got = lax.optimization_barrier((near_side, got))
    far_side = swap(near_side, far)
    for piece in got:
        total = total + piece.astype(f32)
    total = total.astype(bf16)


    projected = total[:, : 3 * head_width].reshape(episodes, horizon, -1)
    grad_heads = total[:, 3 * head_width :]
    head_mix, weights, rounded = jax.vmap(attend)(
        projected, prefix_keys, prefix_values, traj_lengths
    )
    head_rows = head_mix.reshape(rows, -1)
    valid = (jnp.arange(horizon, dtype=jnp.int32)[None, :] < traj_lengths[:, None]).reshape(-1)
    grad_heads = jnp.where(valid[:, None], grad_heads, jnp.zeros_like(grad_heads))
    masked_rows = jnp.where(valid[:, None], head_rows, jnp.zeros_like(head_rows))
    grad_proj = jax.vmap(attend_back)(
        projected,
        prefix_keys,
        prefix_values,
        weights,
        rounded,
        grad_heads.reshape(episodes, horizon, -1),
    ).reshape(rows, -1)


    def wanted(q):
        own, other = q * qkv_part, (q ^ far) * qkv_part
        return (
            (0, own, own + qkv_part),
            (0, other, other + early_width),
            (1, q * out_part, (q + 1) * out_part),
            (1, (q ^ far) * out_part, ((q ^ far) + 1) * out_part),
        )

    parcels = parcel([grad_proj, masked_rows], tuple(wanted(q) for q in range(roles)))
    mine = None
    for q in range(learner):
        got = lax.ppermute(parcels[q], "role", [(learner, q)])
        mine = got if mine is None else mine + got
    mine = jnp.where(is_learner, parcels[learner], mine)
    mine = jnp.concatenate([mine, head_rows], 1)
    moments_out = jnp.concatenate([first_out.astype(bf16), second_out.astype(bf16)], 0)
    far_moments_out = swap(moments_out, far)
    blocks = [mine] + [hop(mine, k) for k in range(1, parts)]
    cuts = [qkv_part, early_width, out_part, out_part, head_width]
    own_rows, far_rows, own_mixed, far_mixed, gathered = stack(blocks, cuts)
    learner_side = jnp.where(role >= far, near_side, far_side)
    learner_inputs = learner_side[:, : inputs.shape[1]]
    learner_cot = learner_side[:, inputs.shape[1] :]

    third = qkv_part - early_width
    high = min(256, first_qkv.shape[0])

    def spots(at, moved, weight):
        return {
            "left": lambda i, j: (0, i),
            "right": lambda i, j: (0, at + j),
            "first": lambda i, j: (i, at + j),
            "second": lambda i, j: (i, at + j + moved),
            "weight": weight,
        }

    late, moment_qkv, square_qkv = update_blocks(
        role, learner_inputs, own_rows, qkv_weight, first_qkv, second_qkv,
        spots(2, 0, lambda i, j, r: (i, r * 3 + 2 + j)), (first_qkv.shape[0], third), (high, third),
    )
    far_late = swap(late, far)
    near_late = swap(late, 1)
    piece_qkv, moment_qkv, square_qkv = update_blocks(
        role, learner_inputs, own_rows, qkv_weight, first_qkv, second_qkv,
        spots(0, 0, lambda i, j, r: (i, r * 3 + j)), (first_qkv.shape[0], early_width), (high, third),
        moments=(moment_qkv, square_qkv),
    )
    late_done = late
    (piece_far,) = update_blocks(
        role, learner_inputs, far_rows, qkv_weight, far_moments, far_moments,
        spots(0, 2, lambda i, j, r: (i, (r ^ far) * 3 + j)), (first_qkv.shape[0], early_width), (high, third), keep=False,
    )
    near_far = swap(piece_far, 1)
    tall = min(256, out_part)
    stories = out_part // tall
    (far_out,) = update_blocks(
        role, far_mixed, learner_cot, out_weight, far_moments_out, far_moments_out,
        {
            **spots(0, 0, lambda i, j, r: ((r ^ far) * stories + i, j)),
            "second": lambda i, j: (i + stories, j),
        },
        (out_part, first_out.shape[1]), (tall, first_out.shape[1]), keep=False,
    )
    piece_out, moment_out, square_out = update_blocks(
        role, own_mixed, learner_cot, out_weight, first_out, second_out,
        spots(0, 0, lambda i, j, r: (r * stories + i, j)), (out_part, first_out.shape[1]), (tall, first_out.shape[1]),
    )
    near_qkv = swap(piece_qkv, 1)
    near_out = swap(piece_out, 1)
    near_far_out = swap(far_out, 1)
    diagonal_late = swap(far_late, 1)
    new_qkv, new_out = join(
        role,
        [piece_qkv, near_qkv, piece_far, near_far],
        [late_done, near_late, far_late, diagonal_late],
        [piece_out, near_out, far_out, near_far_out],
    )

    decoded = turn(jnp.dot(gathered, out_weight, preferred_element_type=f32).astype(bf16))
    return (decoded, new_qkv, new_out, moment_qkv, square_qkv, moment_out, square_out)


def solution(mesh):
    in_specs = (
        P(("role", "shard"), None),
        P(("role", "shard")),
        P(None, "shard"),
        P(("role", "shard"), None, None),
        P(("role", "shard"), None, None),
        P("shard", None),
        P(None, "shard"),
        P("shard", "role"),
        P("shard", "role"),
        P("role", "shard"),
        P("role", "shard"),
        P("role", "shard"),
    )
    out_specs = (
        P("role", "shard"),
        P("shard", None),
        P(None, "shard"),
        P("shard", "role"),
        P("shard", "role"),
        P("role", "shard"),
        P("role", "shard"),
    )
    return jax.shard_map(update, mesh=mesh, in_specs=in_specs, out_specs=out_specs, check_vma=False)
```
